32 devices in a mesh: row: 16 (over z, x, core), col: 2 (over y).
Axes of the slice: x: 2, y: 2, z: 4, core: 2. Of those that a mesh axis runs over, the one named last changes fastest.
Arguments:
- matrix_panel: bfloat16 [128, 131072], P('col', 'row'), may hold values from -6 to 6
- row_signs: int32 [131072], P('row'), may hold values from -1 to 1, as said below
- sample_rows: int32 [2048], replicated, may hold values from 0 to 131071, as said below
Outputs:
- sketch: float32 [128, 2048], P('col', 'row')
- gram: float32 [128, 128], P('col')
The draws below stay inside these ranges and needn't reach their ends.
Inputs may be any that keep to these rules, and one draw needn't show every extreme that they name: `row_signs`: each entry is -1 or +1. `sample_rows`: strictly increasing, so all distinct.
All inputs are finite; a program needn't handle non-finite values.
Results may differ from the reference program's by a relative error of at most 0.0003.
Values sent between devices are 32-bit elements; how exact they have to be, the bound alone decides.
No kernel may reach another device: no remote copies, remote signals or barrier semaphores. Data moves between devices by JAX's collectives and lax.ppermute only.
A program may use at most 64 MiB of HBM per device.

```python
import jax
import jax.numpy as jnp
from jax import lax

PANEL = 128
ROWS_DEV = 8192
LENGTH = 131072
SAMPLES = 2048
N_ROW = 16


def draw_row_signs(key, part):
    return (jax.random.randint(key, (LENGTH,), 0, 2) * 2 - 1).astype(jnp.int32)


def draw_sample_rows(key, part):
    picked = jax.random.choice(jax.random.fold_in(key, 7), LENGTH, (SAMPLES,), replace=False)
    return jnp.sort(picked.astype(jnp.int32))


def levels(own_key, extent, shards, smallest, top_value):
    def one(dim, blocks):
        heights = jax.random.uniform(jax.random.fold_in(jax.random.fold_in(own_key, 6), dim), (blocks,), jnp.float32, smallest / len(shards), top_value / len(shards))
        return jnp.repeat(jnp.exp(heights), extent[dim] // blocks).reshape((-1,) + (1,) * (len(extent) - dim - 1))

    loudness = one(*shards[0])
    for cut in shards[1:]:
        loudness = loudness * one(*cut)
    return loudness


def noise(key, shape, spread, bound, shards=(), kind=jnp.bfloat16):
    factor_of = levels(key, shape, shards, -0.22, 0.18) if shards else 1.0
    result = jax.random.normal(key, shape, jnp.float32) * spread * factor_of
    return jnp.minimum(jnp.maximum(result, -bound), bound).astype(kind)


def setup_inputs(seed: int = 0) -> dict:
    splits = jax.random.split(jax.random.key(seed), 4)
    return {
        "matrix_panel": noise(splits[0], (PANEL, LENGTH), 1.0, 6.0, ((0, 2), (1, 16))),
        "row_signs": draw_row_signs(jax.random.fold_in(splits[3], 71), 0),
        "sample_rows": draw_sample_rows(jax.random.fold_in(splits[3], 71), 0),
    }


def parity_sign(left, right, bit_count):
    common = jnp.bitwise_and(left, right)
    total = jnp.zeros_like(common)
    for bit_index in range(bit_count):
        total = total + jnp.bitwise_and(jnp.right_shift(common, bit_index), 1)
    return (1 - 2 * jnp.bitwise_and(total, 1)).astype(jnp.float32)

def hadamard(order_size):
    bit_count = order_size.bit_length() - 1
    row_index = jnp.arange(order_size, dtype=jnp.int32)
    return parity_sign(row_index[:, None], row_index[None, :], bit_count)

def local_mix(block, signs):
    columns, length = block.shape
    first_size = min(length, 256)
    second_size = length // first_size
    values = block.astype(jnp.float32) * signs.astype(jnp.float32)[None, :]
    values = values.reshape(columns, first_size, second_size)
    values = jnp.einsum('cab,ad->cdb', values, hadamard(first_size), precision=lax.Precision.HIGHEST)
    values = jnp.einsum('cdb,be->cde', values, hadamard(second_size), precision=lax.Precision.HIGHEST)
    return values.reshape(columns, length) / jnp.sqrt(jnp.float32(length))

def reference(matrix_panel, row_signs, sample_rows):
    bit_count = N_ROW.bit_length() - 1
    owner = sample_rows // ROWS_DEV
    offset = sample_rows - owner * ROWS_DEV

    def accumulate(carry, block_index):
        start = (block_index * ROWS_DEV).astype(jnp.int32)
        block = lax.dynamic_slice_in_dim(matrix_panel, start, ROWS_DEV, 1)
        signs = lax.dynamic_slice_in_dim(row_signs, start, ROWS_DEV, 0)
        mixed = local_mix(block, signs)
        chosen = jnp.take(mixed, offset, axis=1)
        weights = parity_sign(owner, block_index, bit_count)
        return (carry + chosen * weights[None, :], None)
    initial = jnp.zeros((PANEL, SAMPLES), jnp.float32)
    summed, _ = lax.scan(accumulate, initial, jnp.arange(N_ROW, dtype=jnp.int32))
    sketch = summed / jnp.sqrt(jnp.float32(N_ROW))
    gram = jnp.dot(sketch, sketch.T, precision=lax.Precision.HIGHEST) / SAMPLES
    return (sketch, gram)
```

```python
import jax
import jax.numpy as jnp
import numpy as np
from jax import lax
from jax.experimental import pallas as pl
from jax.experimental.pallas import tpu as pltpu
from jax.sharding import PartitionSpec as P

WIDE = 256
LANES = 128


def parity(value, bits):
    total = jnp.zeros_like(value)
    for k in range(bits):
        total = total ^ (value >> k)
    return total & 1


def mix_kernel(devices, scale, x_hbm, s_ref, rows_smem, rows_ref, keep_ref, send_ref,
               x_ref, t_ref, g_ref, sems):
    columns, length = x_ref.shape
    blocks = length // WIDE
    slabs = blocks // 2
    per = rows_ref.shape[1]
    bits = devices.bit_length() - 1
    groups = slabs // 2
    span = 2 * WIDE
    half = length // 2
    copies = []
    for g in range(groups):
        for h in range(2):
            window = pl.ds(h * half + g * span, span)
            copies.append(pltpu.make_async_copy(x_hbm.at[:, window], x_ref.at[:, window], sems.at[g, h]))
            copies[-1].start()
    left = lax.broadcasted_iota(jnp.int32, (WIDE, WIDE), 0)
    right = lax.broadcasted_iota(jnp.int32, (WIDE, WIDE), 1)
    mat = (1 - 2 * parity(left & right, WIDE.bit_length() - 1)).astype(jnp.float32).astype(jnp.bfloat16)
    for g in range(groups):
        copies[2 * g].wait()
        copies[2 * g + 1].wait()
        parts = []
        for q in range(2):
            for h in range(2):
                block = h * slabs + 2 * g + q
                signs = jnp.concatenate([s_ref[2 * block:2 * block + 1, :], s_ref[2 * block + 1:2 * block + 2, :]], axis=1)
                parts.append(x_ref[:, block * WIDE:(block + 1) * WIDE] * signs.astype(jnp.float32).astype(jnp.bfloat16))
        stacked = jnp.concatenate(parts, axis=0)
        out = lax.dot_general(mat, stacked, (((1,), (1,)), ((), ())), preferred_element_type=jnp.float32)
        one, two = out[:, :LANES], out[:, LANES:]
        t_ref[(2 * g) * WIDE:(2 * g + 1) * WIDE, :] = one + two
        t_ref[(2 * g + 1) * WIDE:(2 * g + 2) * WIDE, :] = one - two

    def butterfly(i, _):
        for q in range(2):
            at = [pl.ds(pl.multiple_of((2 * g + q) * WIDE + i * 8, 8), 8) for g in range(groups)]
            v = [t_ref[a, :] for a in at]
            step = 1
            while step < groups:
                for j in range(groups):
                    if not j & step:
                        v[j], v[j + step] = v[j] + v[j + step], v[j] - v[j + step]
                step *= 2
            for a, value in zip(at, v):
                t_ref[a, :] = value
        return 0

    lax.fori_loop(0, WIDE // 8, butterfly, 0, unroll=4)

    me = lax.axis_index("row")
    top = length.bit_length() - 2
    for out_ref, base in ((send_ref, devices // 2), (keep_ref, 0)):
        def gather(i, _, out_ref=out_ref, base=base):
            p = base + i
            dest = me
            for k in range(bits):
                dest = dest ^ (((p >> k) & 1) << (bits - 1 - k))
            for t in range(per):
                row = rows_smem[dest * per + t] & (half - 1)
                g_ref[t:t + 1, :] = t_ref[pl.ds(row, 1), :]
            turned = g_ref[...].T
            samples = rows_ref[pl.ds(dest, 1), :]
            flip = parity((samples >> (top + 1)) & me, bits)
            first = jnp.where(flip == 1, -scale, scale)
            second = jnp.where((flip ^ ((samples >> top) & 1)) == 1, -scale, scale)
            out_ref[i] = turned[:columns, :] * first + turned[columns:, :] * second
            return 0
        lax.fori_loop(0, devices // 2, gather, 0)


def mix(matrix_panel, row_signs, sample_rows, devices):
    columns, length = matrix_panel.shape
    per = sample_rows.shape[0] // devices
    scale = float(1.0 / np.sqrt(float(length) * devices))
    vmem = pl.BlockSpec(memory_space=pltpu.VMEM)
    smem = pl.BlockSpec(memory_space=pltpu.SMEM)
    piece = jax.ShapeDtypeStruct((devices // 2, columns, per), jnp.float32)
    return pl.pallas_call(
        lambda *refs: mix_kernel(devices, scale, *refs),
        out_shape=(piece, piece),
        in_specs=[pl.BlockSpec(memory_space=pl.ANY), vmem, smem, vmem],
        out_specs=(vmem, vmem),
        scratch_shapes=[
            pltpu.VMEM((columns, length), jnp.bfloat16),
            pltpu.VMEM((length // 2, LANES), jnp.float32),
            pltpu.VMEM((per, LANES), jnp.float32),
            pltpu.SemaphoreType.DMA((length // WIDE // 4, 2)),
        ],
    )(matrix_panel, row_signs.reshape(length // LANES, LANES), sample_rows, sample_rows.reshape(devices, per))


def flip(value, axis, bit):
    size = lax.axis_size(axis)
    return lax.ppermute(value, axis, [(i, i ^ bit) for i in range(size)])


def body(matrix_panel, row_signs, sample_rows):
    devices = lax.axis_size("row")
    columns, length = matrix_panel.shape
    everything = sample_rows.shape[0]
    per = everything // devices
    bits = devices.bit_length() - 1
    keep, send = mix(matrix_panel, row_signs, sample_rows, devices)
    for k in range(bits):
        total = keep + flip(send, "row", 1 << k)
        if k < bits - 1:
            half = total.shape[0] // 2
            keep, send = total[:half], total[half:]
    sketch = total[0]
    other = flip(sketch, "col", 1)
    own = jnp.dot(sketch, sketch.T, precision=lax.Precision.HIGHEST)
    cross = jnp.dot(sketch, other.T, precision=lax.Precision.HIGHEST)
    first = lax.axis_index("col") == 0
    gram = jnp.concatenate([jnp.where(first, own, cross), jnp.where(first, cross, own)], axis=1)
    gram = gram / everything
    for k in range(bits):
        gram = gram + flip(gram, "row", 1 << k)
    return (sketch, gram)


def solution(mesh):
    return jax.shard_map(
        body,
        mesh=mesh,
        in_specs=(P("col", "row"), P("row"), P()),
        out_specs=(P("col", "row"), P("col", None)),
        check_vma=False,
    )
```

```python
import jax
import jax.numpy as jnp
import numpy as np
from jax import lax
from jax.experimental import pallas as pl
from jax.experimental.pallas import tpu as pltpu
from jax.sharding import PartitionSpec as P

WIDE = 256
LANES = 128
VMEM_GRANT = 16 << 20


def in_hbm(value):
    return pltpu.with_memory_space_constraint(value, pltpu.HBM)


def parity(value, bits):
    total = jnp.zeros_like(value)
    for k in range(bits):
        total = total ^ (value >> k)
    return total & 1


def mix_blocks(x_hbm, s_ref, s_copy, x_ref, t_ref, sems):
    columns, length = x_ref.shape
    slabs = length // WIDE // 2
    groups = slabs // 2
    span = 2 * WIDE
    half = length // 2
    copies = []
    for g in range(groups):
        for h in range(2):
            window = pl.ds(h * half + g * span, span)
            copies.append(pltpu.make_async_copy(x_hbm.at[:, window], x_ref.at[:, window], sems.at[g, h]))
            copies[-1].start()
    left = lax.broadcasted_iota(jnp.int32, (WIDE, WIDE), 0)
    right = lax.broadcasted_iota(jnp.int32, (WIDE, WIDE), 1)
    mat = (1 - 2 * parity(left & right, WIDE.bit_length() - 1)).astype(jnp.float32).astype(jnp.bfloat16)
    s_copy.wait()
    for g in range(groups):
        copies[2 * g].wait()
        copies[2 * g + 1].wait()
        parts = []
        for q in range(2):
            for h in range(2):
                block = h * slabs + 2 * g + q
                signs = jnp.concatenate([s_ref[2 * block:2 * block + 1, :], s_ref[2 * block + 1:2 * block + 2, :]], axis=1)
                parts.append(x_ref[:, block * WIDE:(block + 1) * WIDE] * signs.astype(jnp.float32).astype(jnp.bfloat16))
        stacked = jnp.concatenate(parts, axis=0)
        out = lax.dot_general(mat, stacked, (((1,), (1,)), ((), ())), preferred_element_type=jnp.float32)
        one, two = out[:, :LANES], out[:, LANES:]
        t_ref[(2 * g) * WIDE:(2 * g + 1) * WIDE, :] = one + two
        t_ref[(2 * g + 1) * WIDE:(2 * g + 2) * WIDE, :] = one - two

    def butterfly(i, _):
        for q in range(2):
            at = [pl.ds(pl.multiple_of((2 * g + q) * WIDE + i * 8, 8), 8) for g in range(groups)]
            v = [t_ref[a, :] for a in at]
            step = 1
            while step < groups:
                for j in range(groups):
                    if not j & step:
                        v[j], v[j + step] = v[j] + v[j + step], v[j] - v[j + step]
                step *= 2
            for a, value in zip(at, v):
                t_ref[a, :] = value
        return 0

    lax.fori_loop(0, WIDE // 8, butterfly, 0, unroll=4)


def gather_blocks(devices, length, columns, base, rows_smem, rows_ref, t_ref, g_ref, out_ref):
    per = rows_ref.shape[1]
    half = length // 2
    bits = devices.bit_length() - 1
    top = length.bit_length() - 2
    scale = float(1.0 / np.sqrt(float(length) * devices))
    me = lax.axis_index("row")

    def gather(i, _):
        p = base + i
        dest = (me & -2) ^ (p & 1)
        for k in range(1, bits):
            dest = dest ^ (((p >> k) & 1) << (bits - k))
        for t in range(per):
            row = rows_smem[dest * per + t] & (half - 1)
            g_ref[t:t + 1, :] = t_ref[pl.ds(row, 1), :]
        turned = g_ref[...].T
        samples = rows_ref[pl.ds(dest, 1), :]
        flip = parity((samples >> (top + 1)) & me, bits)
        first = jnp.where(flip == 1, -scale, scale)
        second = jnp.where((flip ^ ((samples >> top) & 1)) == 1, -scale, scale)
        out_ref[i] = turned[:columns, :] * first + turned[columns:, :] * second
        return 0

    lax.fori_loop(0, out_ref.shape[0], gather, 0)


def mix(matrix_panel, row_signs, sample_rows, devices):
    columns, length = matrix_panel.shape
    per = sample_rows.shape[0] // devices
    half = devices // 2
    anywhere = pl.BlockSpec(memory_space=pltpu.HBM)

    def kernel(x_hbm, s_hbm, flat_hbm, rows_hbm, t_ref, out_ref, x_ref, s_ref, flat_ref, rows_ref, g_ref, sems, more):
        fetch = [pltpu.make_async_copy(a, b, more.at[k]) for k, (a, b) in enumerate(((s_hbm, s_ref), (flat_hbm, flat_ref), (rows_hbm, rows_ref)))]
        for copy in fetch:
            copy.start()
        mix_blocks(x_hbm, s_ref, fetch[0], x_ref, t_ref, sems)
        fetch[1].wait()
        fetch[2].wait()
        gather_blocks(devices, length, columns, half, flat_ref, rows_ref, t_ref, g_ref, out_ref)

    return pl.pallas_call(
        kernel,
        out_shape=(pltpu.VMEM((length // 2, LANES), jnp.float32), pltpu.VMEM((half, columns, per), jnp.float32)),
        in_specs=[anywhere] * 4,
        scratch_shapes=[
            pltpu.VMEM((columns, length), jnp.bfloat16),
            pltpu.VMEM((length // LANES, LANES), jnp.int32),
            pltpu.SMEM(sample_rows.shape, jnp.int32),
            pltpu.VMEM((devices, per), jnp.int32),
            pltpu.VMEM((per, LANES), jnp.float32),
            pltpu.SemaphoreType.DMA((length // WIDE // 4, 2)),
            pltpu.SemaphoreType.DMA((3,)),
        ],
        compiler_params=pltpu.CompilerParams(vmem_limit_bytes=VMEM_GRANT),
    )(*(in_hbm(a) for a in (matrix_panel, row_signs.reshape(length // LANES, LANES), sample_rows, sample_rows.reshape(devices, per))))


def pick(table, sample_rows, columns, length, devices):
    per = sample_rows.shape[0] // devices
    half = devices // 2
    anywhere = pl.BlockSpec(memory_space=pltpu.HBM)

    def kernel(t_ref, flat_hbm, rows_hbm, out_ref, flat_ref, rows_ref, g_ref, more):
        fetch = [pltpu.make_async_copy(a, b, more.at[k]) for k, (a, b) in enumerate(((flat_hbm, flat_ref), (rows_hbm, rows_ref)))]
        for copy in fetch:
            copy.start()
        for copy in fetch:
            copy.wait()
        gather_blocks(devices, length, columns, 0, flat_ref, rows_ref, t_ref, g_ref, out_ref)

    return pl.pallas_call(
        kernel,
        out_shape=pltpu.VMEM((half, columns, per), jnp.float32),
        in_specs=[pl.BlockSpec(memory_space=pltpu.VMEM), anywhere, anywhere],
        scratch_shapes=[
            pltpu.SMEM(sample_rows.shape, jnp.int32),
            pltpu.VMEM((devices, per), jnp.int32),
            pltpu.VMEM((per, LANES), jnp.float32),
            pltpu.SemaphoreType.DMA((2,)),
        ],
        compiler_params=pltpu.CompilerParams(vmem_limit_bytes=VMEM_GRANT),
    )(pltpu.with_memory_space_constraint(table, pltpu.VMEM), in_hbm(sample_rows), in_hbm(sample_rows.reshape(devices, per)))


def chips(value, bit):
    size = lax.axis_size("row")
    return lax.ppermute(value, "row", [(i, i ^ bit) for i in range(1, size, 2)])


def up(value):
    return lax.ppermute(value, "row", [(i, i + 1) for i in range(0, lax.axis_size("row"), 2)])


def down(value):
    return lax.ppermute(value, "row", [(i + 1, i) for i in range(0, lax.axis_size("row"), 2)])


def body(matrix_panel, row_signs, sample_rows):
    devices = lax.axis_size("row")
    columns, length = matrix_panel.shape
    everything = sample_rows.shape[0]
    bits = devices.bit_length() - 1
    odd = (lax.axis_index("row") & 1) == 1
    table, send = mix(matrix_panel, row_signs, sample_rows, devices)
    send = send + up(send)
    table, send = lax.optimization_barrier((table, send))
    moved = chips(send, 2)
    keep = pick(table, sample_rows, columns, length, devices)
    total = (keep + up(keep)) + moved
    for k in range(2, bits - 1):
        half = total.shape[0] // 2
        total = total[:half] + chips(total[half:], 1 << k)
    moved = chips(total, 1 << (bits - 1))
    mine = total[:2] + moved[2:]
    theirs = total[2:] + moved[:2]
    full = jnp.concatenate([mine, theirs], axis=0)
    pairs = [((2 * i + 1) * 2 + c, (2 * i + 1) * 2 + 1 - c) for i in range(devices // 2) for c in range(2)]
    other = lax.ppermute(full, ("row", "col"), pairs)
    sketch = jnp.where(odd, mine[1], down(mine[0]))
    own = jnp.einsum("bcs,bds->cd", full, full, precision=lax.Precision.HIGHEST)
    cross = jnp.einsum("bcs,bds->cd", full, other, precision=lax.Precision.HIGHEST)
    first = lax.axis_index("col") == 0
    gram = jnp.concatenate([jnp.where(first, own, cross), jnp.where(first, cross, own)], axis=1)
    gram = gram / everything
    for k in range(1, bits - 1):
        gram = gram + chips(gram, 1 << k)
    gram = jnp.where(odd, gram, down(gram))
    return (sketch, gram)


def solution(mesh):
    return jax.shard_map(
        body,
        mesh=mesh,
        in_specs=(P("col", "row"), P("row"), P()),
        out_specs=(P("col", "row"), P("col", None)),
        check_vma=False,
    )
```

```python
import jax
import jax.numpy as jnp
import numpy as np
from jax import lax
from jax.experimental import pallas as pl
from jax.experimental.pallas import tpu as pltpu
from jax.sharding import PartitionSpec as P


WIDE = 256
LANES = 128
VMEM_GRANT = 16 << 20


def in_hbm(value):
    return pltpu.with_memory_space_constraint(value, pltpu.HBM)


def parity(value, bits):
    total = jnp.zeros_like(value)
    for k in range(bits):
        total = total ^ (value >> k)
    return total & 1


def mix_blocks(x_hbm, s_ref, s_copy, x_ref, t_ref, sems):
    _, length = x_ref.shape
    slabs = length // WIDE // 2
    groups = slabs // 2
    span = 2 * WIDE
    half = length // 2
    copies = []
    for g in range(groups):
        for h in range(2):
            window = pl.ds(h * half + g * span, span)
            copies.append(pltpu.make_async_copy(x_hbm.at[:, window], x_ref.at[:, window], sems.at[g, h]))
            copies[-1].start()
    left = lax.broadcasted_iota(jnp.int32, (WIDE, WIDE), 0)
    right = lax.broadcasted_iota(jnp.int32, (WIDE, WIDE), 1)
    mat = (1 - 2 * parity(left & right, WIDE.bit_length() - 1)).astype(jnp.float32).astype(jnp.bfloat16)
    s_copy.wait()
    for g in range(groups):
        copies[2 * g].wait()
        copies[2 * g + 1].wait()
        parts = []
        for q in range(2):
            for h in range(2):
                block = h * slabs + 2 * g + q
                signs = jnp.concatenate([s_ref[2 * block:2 * block + 1, :], s_ref[2 * block + 1:2 * block + 2, :]], axis=1)
                parts.append(x_ref[:, block * WIDE:(block + 1) * WIDE] * signs.astype(jnp.float32).astype(jnp.bfloat16))
        stacked = jnp.concatenate(parts, axis=0)
        out = lax.dot_general(mat, stacked, (((1,), (1,)), ((), ())), preferred_element_type=jnp.float32)
        one, two = out[:, :LANES], out[:, LANES:]
        t_ref[(2 * g) * WIDE:(2 * g + 1) * WIDE, :] = one + two
        t_ref[(2 * g + 1) * WIDE:(2 * g + 2) * WIDE, :] = one - two

    def butterfly(i, _):
        for q in range(2):
            at = [pl.ds(pl.multiple_of((2 * g + q) * WIDE + i * 8, 8), 8) for g in range(groups)]
            v = [t_ref[a, :] for a in at]
            step = 1
            while step < groups:
                for j in range(groups):
                    if not j & step:
                        v[j], v[j + step] = v[j] + v[j + step], v[j] - v[j + step]
                step *= 2
            for a, value in zip(at, v):
                t_ref[a, :] = value
        return 0

    lax.fori_loop(0, WIDE // 8, butterfly, 0, unroll=4)


def step_of(k):
    return (1 << k) | 1


def gather_blocks(devices, length, columns, corner, rows_smem, rows_ref, t_ref, g_ref, out_ref):
    per = rows_ref.shape[1]
    half = length // 2
    bits = devices.bit_length() - 1
    top = length.bit_length() - 2
    scale = float(1.0 / np.sqrt(float(length) * devices))
    me = lax.axis_index("row")

    def gather(i, _):
        dest = me ^ corner
        for k in range(2, bits):
            dest = dest ^ (((i >> (bits - 1 - k)) & 1) * step_of(k))
        for t in range(per):
            row = rows_smem[dest * per + t] & (half - 1)
            g_ref[t:t + 1, :] = t_ref[pl.ds(row, 1), :]
        turned = g_ref[...].T
        samples = rows_ref[pl.ds(dest, 1), :]
        flip = parity((samples >> (top + 1)) & me, bits)
        first = jnp.where(flip == 1, -scale, scale)
        second = jnp.where((flip ^ ((samples >> top) & 1)) == 1, -scale, scale)
        out_ref[i] = turned[:columns, :] * first + turned[columns:, :] * second
        return 0

    lax.fori_loop(0, out_ref.shape[0], gather, 0)


def corner_of(c0, c1):
    return c0 * step_of(0) ^ c1 * step_of(1)


def mix(matrix_panel, row_signs, sample_rows, devices, corner):
    columns, length = matrix_panel.shape
    per = sample_rows.shape[0] // devices
    hbm = pl.BlockSpec(memory_space=pltpu.HBM)

    def kernel(x_hbm, s_hbm, flat_hbm, rows_hbm, t_ref, out_ref, x_ref, s_ref, flat_ref, rows_ref, g_ref, sems, more):
        fetch = [pltpu.make_async_copy(a, b, more.at[k]) for k, (a, b) in enumerate(((s_hbm, s_ref), (flat_hbm, flat_ref), (rows_hbm, rows_ref)))]
        for copy in fetch:
            copy.start()
        mix_blocks(x_hbm, s_ref, fetch[0], x_ref, t_ref, sems)
        fetch[1].wait()
        fetch[2].wait()
        gather_blocks(devices, length, columns, corner, flat_ref, rows_ref, t_ref, g_ref, out_ref)

    return pl.pallas_call(
        kernel,
        out_shape=(pltpu.VMEM((length // 2, LANES), jnp.float32), pltpu.VMEM((devices // 4, columns, per), jnp.float32)),
        in_specs=[hbm] * 4,
        scratch_shapes=[
            pltpu.VMEM((columns, length), jnp.bfloat16),
            pltpu.VMEM((length // LANES, LANES), jnp.int32),
            pltpu.SMEM(sample_rows.shape, jnp.int32),
            pltpu.VMEM((devices, per), jnp.int32),
            pltpu.VMEM((per, LANES), jnp.float32),
            pltpu.SemaphoreType.DMA((length // WIDE // 4, 2)),
            pltpu.SemaphoreType.DMA((3,)),
        ],
        compiler_params=pltpu.CompilerParams(vmem_limit_bytes=VMEM_GRANT),
    )(*(in_hbm(a) for a in (matrix_panel, row_signs.reshape(length // LANES, LANES), sample_rows, sample_rows.reshape(devices, per))))


def pick(table, sample_rows, columns, length, devices, corner):
    per = sample_rows.shape[0] // devices
    hbm = pl.BlockSpec(memory_space=pltpu.HBM)

    def kernel(t_ref, flat_hbm, rows_hbm, out_ref, flat_ref, rows_ref, g_ref, more):
        fetch = [pltpu.make_async_copy(a, b, more.at[k]) for k, (a, b) in enumerate(((flat_hbm, flat_ref), (rows_hbm, rows_ref)))]
        for copy in fetch:
            copy.start()
        for copy in fetch:
            copy.wait()
        gather_blocks(devices, length, columns, corner, flat_ref, rows_ref, t_ref, g_ref, out_ref)

    return pl.pallas_call(
        kernel,
        out_shape=pltpu.VMEM((devices // 4, columns, per), jnp.float32),
        in_specs=[pl.BlockSpec(memory_space=pltpu.VMEM), hbm, hbm],
        scratch_shapes=[
            pltpu.SMEM(sample_rows.shape, jnp.int32),
            pltpu.VMEM((devices, per), jnp.int32),
            pltpu.VMEM((per, LANES), jnp.float32),
            pltpu.SemaphoreType.DMA((2,)),
        ],
        compiler_params=pltpu.CompilerParams(vmem_limit_bytes=VMEM_GRANT),
    )(pltpu.with_memory_space_constraint(table, pltpu.VMEM), in_hbm(sample_rows), in_hbm(sample_rows.reshape(devices, per)))


def products(full, other, everything):
    blocks, columns, _ = full.shape

    def kernel(a_ref, b_ref, o_ref):
        own = jnp.zeros((columns, columns), jnp.float32)
        cross = jnp.zeros((columns, columns), jnp.float32)
        dims = (((1,), (1,)), ((), ()))
        for i in range(blocks):
            own = own + lax.dot_general(a_ref[i], a_ref[i], dims, precision=lax.Precision.HIGHEST)
            cross = cross + lax.dot_general(a_ref[i], b_ref[i], dims, precision=lax.Precision.HIGHEST)
        first = lax.axis_index("col") == 0
        both = jnp.concatenate([jnp.where(first, own, cross), jnp.where(first, cross, own)], axis=1)
        o_ref[...] = both * (1.0 / everything)

    vmem = pl.BlockSpec(memory_space=pltpu.VMEM)
    return pl.pallas_call(
        kernel,
        out_shape=pltpu.VMEM((columns, 2 * columns), jnp.float32),
        in_specs=[vmem, vmem],
        compiler_params=pltpu.CompilerParams(vmem_limit_bytes=VMEM_GRANT),
    )(pltpu.with_memory_space_constraint(full, pltpu.VMEM), pltpu.with_memory_space_constraint(other, pltpu.VMEM))


def swap(value, k):
    return lax.ppermute(value, "row", [(i, i ^ step_of(k)) for i in range(lax.axis_size("row"))])


def body(matrix_panel, row_signs, sample_rows):
    devices = lax.axis_size("row")
    columns, length = matrix_panel.shape
    everything = sample_rows.shape[0]
    bits = devices.bit_length() - 1

    def part(table, c0, c1):
        return pick(table, sample_rows, columns, length, devices, corner_of(c0, c1))

    table, far = mix(matrix_panel, row_signs, sample_rows, devices, corner_of(1, 1))
    send = part(table, 0, 1) + swap(far, 0)
    table, send = lax.optimization_barrier((table, send))
    moved = swap(send, 1)
    far = part(table, 1, 0)
    near = swap(far, 0)
    table, far = lax.optimization_barrier((table, far))
    rest = part(table, 0, 0)
    total = (rest + near) + moved
    for k in range(2, bits - 1):
        half = total.shape[0] // 2
        total = total[:half] + swap(total[half:], k)
    moved = swap(total, bits - 1)
    mine = total[:1] + moved[1:]
    theirs = total[1:] + moved[:1]
    full = jnp.concatenate([mine, theirs], axis=0)
    other = lax.ppermute(full, "col", [(0, 1), (1, 0)])
    gram = products(full, other, everything)
    for k in range(bits - 1):
        gram = gram + swap(gram, k)
    return (mine[0], gram)


def solution(mesh):
    return jax.shard_map(
        body,
        mesh=mesh,
        in_specs=(P("col", "row"), P("row"), P()),
        out_specs=(P("col", "row"), P("col", None)),
        check_vma=False,
    )
```

```python
import jax
import jax.numpy as jnp
import numpy as np
from jax import lax
from jax.experimental import pallas as pl
from jax.experimental.pallas import tpu as pltpu
from jax.sharding import PartitionSpec as P


WIDE = 256
LANES = 128
VMEM_GRANT = 16 << 20
CHUNKS = 1
SLOTS = 4


def in_space(value, space):
    return pltpu.with_memory_space_constraint(value, space)


def parity(value, bits):
    total = jnp.zeros_like(value)
    for k in range(bits):
        total = total ^ (value >> k)
    return total & 1


def mix_blocks(x_hbm, s_ref, s_copy, x_ref, t_ref, sems):
    _, length = x_ref.shape
    slabs = length // WIDE // 2
    groups = slabs // 2
    span = 2 * WIDE
    half = length // 2
    copies = []
    chunk = groups * span // CHUNKS
    for g in range(CHUNKS):
        for h in range(2):
            window = pl.ds(h * half + g * chunk, chunk)
            copies.append(pltpu.make_async_copy(x_hbm.at[:, window], x_ref.at[:, window], sems.at[g, h]))
            copies[-1].start()
    left = lax.broadcasted_iota(jnp.int32, (WIDE, WIDE), 0)
    right = lax.broadcasted_iota(jnp.int32, (WIDE, WIDE), 1)
    mat = (1 - 2 * parity(left & right, WIDE.bit_length() - 1)).astype(jnp.float32).astype(jnp.bfloat16)
    s_copy.wait()
    for g in range(groups):
        if g % (groups // CHUNKS) == 0:
            first = g // (groups // CHUNKS)
            copies[2 * first].wait()
            copies[2 * first + 1].wait()
        parts = []
        for q in range(2):
            for h in range(2):
                block = h * slabs + 2 * g + q
                signs = jnp.concatenate([s_ref[2 * block:2 * block + 1, :], s_ref[2 * block + 1:2 * block + 2, :]], axis=1)
                parts.append(x_ref[:, block * WIDE:(block + 1) * WIDE] * signs.astype(jnp.float32).astype(jnp.bfloat16))
        stacked = jnp.concatenate(parts, axis=0)
        out = lax.dot_general(mat, stacked, (((1,), (1,)), ((), ())), preferred_element_type=jnp.float32)
        one, two = out[:, :LANES], out[:, LANES:]
        t_ref[(2 * g) * WIDE:(2 * g + 1) * WIDE, :] = one + two
        t_ref[(2 * g + 1) * WIDE:(2 * g + 2) * WIDE, :] = one - two

    def butterfly(i, _):
        for q in range(2):
            at = [pl.ds(pl.multiple_of((2 * g + q) * WIDE + i * 8, 8), 8) for g in range(groups)]
            v = [t_ref[a, :] for a in at]
            step = 1
            while step < groups:
                for j in range(groups):
                    if not j & step:
                        v[j], v[j + step] = v[j] + v[j + step], v[j] - v[j + step]
                step *= 2
            for a, value in zip(at, v):
                t_ref[a, :] = value
        return 0

    lax.fori_loop(0, WIDE // 8, butterfly, 0, unroll=4)


def step_of(k):
    return (1 << k) | 1


def gather_blocks(devices, length, columns, corner, rows_smem, rows_ref, t_ref, g_ref, out_ref):
    per = rows_ref.shape[1]
    half = length // 2
    bits = devices.bit_length() - 1
    top = length.bit_length() - 2
    scale = float(1.0 / np.sqrt(float(length) * devices))
    me = lax.axis_index("row")

    def gather(i, slot):
        dest = me ^ corner
        for k in range(2, bits):
            dest = dest ^ (((i >> (bits - 1 - k)) & 1) * step_of(k))
        for t in range(per):
            row = rows_smem[dest * per + t] & (half - 1)
            g_ref[slot][t:t + 1, :] = t_ref[pl.ds(row, 1), :]
        turned = g_ref[slot][...].T
        samples = rows_ref[pl.ds(dest, 1), :]
        flip = parity((samples >> (top + 1)) & me, bits)
        first = jnp.where(flip == 1, -scale, scale)
        second = jnp.where((flip ^ ((samples >> top) & 1)) == 1, -scale, scale)
        out_ref[i] = turned[:columns, :] * first + turned[columns:, :] * second

    def several(j, _):
        for slot in range(SLOTS):
            gather(j * SLOTS + slot, slot)
        return 0

    lax.fori_loop(0, out_ref.shape[0] // SLOTS, several, 0)


def corner_of(c0, c1):
    return c0 * step_of(0) ^ c1 * step_of(1)


def mix(matrix_panel, row_signs, sample_rows, devices, corner):
    columns, length = matrix_panel.shape
    per = sample_rows.shape[0] // devices
    hbm, vmem, smem = (pl.BlockSpec(memory_space=m) for m in (pltpu.HBM, pltpu.VMEM, pltpu.SMEM))

    def kernel(x_hbm, s_hbm, flat_hbm, rows_hbm, t_ref, out_ref, flat_ref, rows_ref, x_ref, s_ref, *rest):
        g_ref, (sems, more) = rest[:SLOTS], rest[SLOTS:]
        fetch = [pltpu.make_async_copy(a, b, more.at[k]) for k, (a, b) in enumerate(((s_hbm, s_ref), (flat_hbm, flat_ref), (rows_hbm, rows_ref)))]
        for copy in fetch:
            copy.start()
        mix_blocks(x_hbm, s_ref, fetch[0], x_ref, t_ref, sems)
        fetch[1].wait()
        fetch[2].wait()
        gather_blocks(devices, length, columns, corner, flat_ref, rows_ref, t_ref, g_ref, out_ref)

    return pl.pallas_call(
        kernel,
        out_shape=(
            pltpu.VMEM((length // 2, LANES), jnp.float32),
            pltpu.VMEM((devices // 4, columns, per), jnp.float32),
            pltpu.SMEM(sample_rows.shape, jnp.int32),
            pltpu.VMEM((devices, per), jnp.int32),
        ),
        in_specs=[hbm] * 4,
        out_specs=(vmem, vmem, smem, vmem),
        scratch_shapes=[
            pltpu.VMEM((columns, length), jnp.bfloat16),
            pltpu.VMEM((length // LANES, LANES), jnp.int32),
            *[pltpu.VMEM((per, LANES), jnp.float32)] * SLOTS,
            pltpu.SemaphoreType.DMA((CHUNKS, 2)),
            pltpu.SemaphoreType.DMA((3,)),
        ],
        compiler_params=pltpu.CompilerParams(vmem_limit_bytes=VMEM_GRANT),
    )(*(in_space(a, pltpu.HBM) for a in (matrix_panel, row_signs.reshape(length // LANES, LANES), sample_rows, sample_rows.reshape(devices, per))))


def pick(table, flat, rows, columns, corner):
    devices, per = rows.shape
    vmem, smem = pl.BlockSpec(memory_space=pltpu.VMEM), pl.BlockSpec(memory_space=pltpu.SMEM)
    length = 2 * table.shape[0]

    def kernel(t_ref, flat_ref, rows_ref, out_ref, *g_ref):
        gather_blocks(devices, length, columns, corner, flat_ref, rows_ref, t_ref, g_ref, out_ref)

    return pl.pallas_call(
        kernel,
        out_shape=pltpu.VMEM((devices // 4, columns, per), jnp.float32),
        in_specs=[vmem, smem, vmem],
        scratch_shapes=[pltpu.VMEM((per, LANES), jnp.float32)] * SLOTS,
        compiler_params=pltpu.CompilerParams(vmem_limit_bytes=VMEM_GRANT),
    )(in_space(table, pltpu.VMEM), in_space(flat, pltpu.SMEM), in_space(rows, pltpu.VMEM))


def products(full, other, everything):
    blocks, columns, _ = full.shape

    def kernel(a_ref, b_ref, o_ref):
        own = jnp.zeros((columns, columns), jnp.float32)
        cross = jnp.zeros((columns, columns), jnp.float32)
        dims = (((1,), (1,)), ((), ()))
        for i in range(blocks):
            own = own + lax.dot_general(a_ref[i], a_ref[i], dims, precision=lax.Precision.HIGHEST)
            cross = cross + lax.dot_general(a_ref[i], b_ref[i], dims, precision=lax.Precision.HIGHEST)
        first = lax.axis_index("col") == 0
        both = jnp.concatenate([jnp.where(first, own, cross), jnp.where(first, cross, own)], axis=1)
        o_ref[...] = both * (1.0 / everything)

    vmem = pl.BlockSpec(memory_space=pltpu.VMEM)
    return pl.pallas_call(
        kernel,
        out_shape=pltpu.VMEM((columns, 2 * columns), jnp.float32),
        in_specs=[vmem, vmem],
        compiler_params=pltpu.CompilerParams(vmem_limit_bytes=VMEM_GRANT),
    )(in_space(full, pltpu.VMEM), in_space(other, pltpu.VMEM))


def swap(value, k):
    return lax.ppermute(value, "row", [(i, i ^ step_of(k)) for i in range(lax.axis_size("row"))])


def body(matrix_panel, row_signs, sample_rows):
    devices = lax.axis_size("row")
    columns, _ = matrix_panel.shape
    everything = sample_rows.shape[0]
    bits = devices.bit_length() - 1

    def part(table, c0, c1):
        return pick(table, flat, rows, columns, corner_of(c0, c1))

    table, far, flat, rows = mix(matrix_panel, row_signs, sample_rows, devices, corner_of(1, 1))
    send = part(table, 0, 1) + swap(far, 0)
    table, send = lax.optimization_barrier((table, send))
    moved = swap(send, 1)
    far = part(table, 1, 0)
    near = swap(far, 0)
    table, far = lax.optimization_barrier((table, far))
    rest = part(table, 0, 0)
    total = (rest + near) + moved
    for k in range(2, bits - 1):
        half = total.shape[0] // 2
        total = total[:half] + swap(total[half:], k)
    moved = swap(total, bits - 1)
    mine = total[:1] + moved[1:]
    theirs = total[1:] + moved[:1]
    full = jnp.concatenate([mine, theirs], axis=0)
    other = lax.ppermute(full, "col", [(0, 1), (1, 0)])
    gram = products(full, other, everything)
    for k in range(bits - 1):
        gram = gram + swap(gram, k)
    return (mine[0], gram)


def solution(mesh):
    return jax.shard_map(
        body,
        mesh=mesh,
        in_specs=(P("col", "row"), P("row"), P()),
        out_specs=(P("col", "row"), P("col", None)),
        check_vma=False,
    )
```

```python
import jax
import jax.numpy as jnp
import numpy as np
from jax import lax
from jax.experimental import pallas as pl
from jax.experimental.pallas import tpu as pltpu
from jax.sharding import PartitionSpec as P


WIDE = 256
LANES = 128
VMEM_GRANT = 16 << 20
CHUNKS = 1
SLOTS = 4


def in_space(value, space):
    return pltpu.with_memory_space_constraint(value, space)


def parity(value, bits):
    total = jnp.zeros_like(value)
    for k in range(bits):
        total = total ^ (value >> k)
    return total & 1


def mix_blocks(x_hbm, s_ref, s_copy, x_ref, t_ref, sems):
    _, length = x_ref.shape
    slabs = length // WIDE // 2
    groups = slabs // 2
    span = 2 * WIDE
    half = length // 2
    copies = []
    chunk = groups * span // CHUNKS
    for g in range(CHUNKS):
        for h in range(2):
            window = pl.ds(h * half + g * chunk, chunk)
            copies.append(pltpu.make_async_copy(x_hbm.at[:, window], x_ref.at[:, window], sems.at[g, h]))
            copies[-1].start()
    left = lax.broadcasted_iota(jnp.int32, (WIDE, WIDE), 0)
    right = lax.broadcasted_iota(jnp.int32, (WIDE, WIDE), 1)
    mat = (1 - 2 * parity(left & right, WIDE.bit_length() - 1)).astype(jnp.float32).astype(jnp.bfloat16)
    s_copy.wait()
    for g in range(groups):
        if g % (groups // CHUNKS) == 0:
            first = g // (groups // CHUNKS)
            copies[2 * first].wait()
            copies[2 * first + 1].wait()
        parts = []
        for q in range(2):
            for h in range(2):
                block = h * slabs + 2 * g + q
                signs = jnp.concatenate([s_ref[2 * block:2 * block + 1, :], s_ref[2 * block + 1:2 * block + 2, :]], axis=1)
                parts.append(x_ref[:, block * WIDE:(block + 1) * WIDE] * signs.astype(jnp.float32).astype(jnp.bfloat16))
        stacked = jnp.concatenate(parts, axis=0)
        out = lax.dot_general(mat, stacked, (((1,), (1,)), ((), ())), preferred_element_type=jnp.float32)
        one, two = out[:, :LANES], out[:, LANES:]
        t_ref[(2 * g) * WIDE:(2 * g + 1) * WIDE, :] = one + two
        t_ref[(2 * g + 1) * WIDE:(2 * g + 2) * WIDE, :] = one - two

    def butterfly(i, _):
        for q in range(2):
            at = [pl.ds(pl.multiple_of((2 * g + q) * WIDE + i * 8, 8), 8) for g in range(groups)]
            v = [t_ref[a, :] for a in at]
            step = 1
            while step < groups:
                for j in range(groups):
                    if not j & step:
                        v[j], v[j + step] = v[j] + v[j + step], v[j] - v[j + step]
                step *= 2
            for a, value in zip(at, v):
                t_ref[a, :] = value
        return 0

    lax.fori_loop(0, WIDE // 8, butterfly, 0, unroll=4)


def step_of(k):
    return (1 << k) | 1


def gather_blocks(devices, length, columns, corner, rows_smem, rows_ref, t_ref, g_ref, out_ref):
    per = rows_ref.shape[1]
    half = length // 2
    bits = devices.bit_length() - 1
    top = length.bit_length() - 2
    scale = float(1.0 / np.sqrt(float(length) * devices))
    me = lax.axis_index("row")

    def gather(i, slot):
        dest = me ^ corner
        for k in range(2, bits):
            dest = dest ^ (((i >> (bits - 1 - k)) & 1) * step_of(k))
        for t in range(per):
            row = rows_smem[dest * per + t] & (half - 1)
            g_ref[slot][t:t + 1, :] = t_ref[pl.ds(row, 1), :]
        turned = g_ref[slot][...].T
        samples = rows_ref[pl.ds(dest, 1), :]
        flip = parity((samples >> (top + 1)) & me, bits)
        first = jnp.where(flip == 1, -scale, scale)
        second = jnp.where((flip ^ ((samples >> top) & 1)) == 1, -scale, scale)
        out_ref[i] = turned[:columns, :] * first + turned[columns:, :] * second

    def several(j, _):
        for slot in range(SLOTS):
            gather(j * SLOTS + slot, slot)
        return 0

    lax.fori_loop(0, out_ref.shape[0] // SLOTS, several, 0)


def corner_of(c0, c1):
    return c0 * step_of(0) ^ c1 * step_of(1)


def mix(matrix_panel, row_signs, sample_rows, devices, corner):
    columns, length = matrix_panel.shape
    per = sample_rows.shape[0] // devices
    hbm, vmem, smem = (pl.BlockSpec(memory_space=m) for m in (pltpu.HBM, pltpu.VMEM, pltpu.SMEM))

    def kernel(x_hbm, s_hbm, flat_hbm, rows_hbm, t_ref, out_ref, flat_ref, rows_ref, x_ref, s_ref, *rest):
        g_ref, (sems, more) = rest[:SLOTS], rest[SLOTS:]
        fetch = [pltpu.make_async_copy(a, b, more.at[k]) for k, (a, b) in enumerate(((s_hbm, s_ref), (flat_hbm, flat_ref), (rows_hbm, rows_ref)))]
        for copy in fetch:
            copy.start()
        mix_blocks(x_hbm, s_ref, fetch[0], x_ref, t_ref, sems)
        fetch[1].wait()
        fetch[2].wait()
        gather_blocks(devices, length, columns, corner, flat_ref, rows_ref, t_ref, g_ref, out_ref)

    return pl.pallas_call(
        kernel,
        out_shape=(
            pltpu.VMEM((length // 2, LANES), jnp.float32),
            pltpu.VMEM((devices // 4, columns, per), jnp.float32),
            pltpu.SMEM(sample_rows.shape, jnp.int32),
            pltpu.VMEM((devices, per), jnp.int32),
        ),
        in_specs=[hbm] * 4,
        out_specs=(vmem, vmem, smem, vmem),
        scratch_shapes=[
            pltpu.VMEM((columns, length), jnp.bfloat16),
            pltpu.VMEM((length // LANES, LANES), jnp.int32),
            *[pltpu.VMEM((per, LANES), jnp.float32)] * SLOTS,
            pltpu.SemaphoreType.DMA((CHUNKS, 2)),
            pltpu.SemaphoreType.DMA((3,)),
        ],
        compiler_params=pltpu.CompilerParams(vmem_limit_bytes=VMEM_GRANT),
    )(*(in_space(a, pltpu.HBM) for a in (matrix_panel, row_signs.reshape(length // LANES, LANES), sample_rows, sample_rows.reshape(devices, per))))


def pick(table, flat, rows, columns, corner):
    devices, per = rows.shape
    vmem, smem = pl.BlockSpec(memory_space=pltpu.VMEM), pl.BlockSpec(memory_space=pltpu.SMEM)
    length = 2 * table.shape[0]

    def kernel(t_ref, flat_ref, rows_ref, out_ref, *g_ref):
        gather_blocks(devices, length, columns, corner, flat_ref, rows_ref, t_ref, g_ref, out_ref)

    return pl.pallas_call(
        kernel,
        out_shape=pltpu.VMEM((devices // 4, columns, per), jnp.float32),
        in_specs=[vmem, smem, vmem],
        scratch_shapes=[pltpu.VMEM((per, LANES), jnp.float32)] * SLOTS,
        compiler_params=pltpu.CompilerParams(vmem_limit_bytes=VMEM_GRANT),
    )(in_space(table, pltpu.VMEM), in_space(flat, pltpu.SMEM), in_space(rows, pltpu.VMEM))


def times(left, right):
    return lax.dot_general(left, right, (((1,), (1,)), ((), ())), precision=lax.Precision.HIGHEST)


def on_chip(kernel, shape, *operands):
    return pl.pallas_call(
        kernel,
        out_shape=pltpu.VMEM(shape, jnp.float32),
        in_specs=[pl.BlockSpec(memory_space=pltpu.VMEM)] * len(operands),
        compiler_params=pltpu.CompilerParams(vmem_limit_bytes=VMEM_GRANT),
    )(*(in_space(a, pltpu.VMEM) for a in operands))


def square(mine):
    def kernel(a_ref, o_ref):
        o_ref[...] = times(a_ref[...], a_ref[...])

    return on_chip(kernel, (mine.shape[0], mine.shape[0]), mine)


def products(own, mine, theirs, other_mine, other_theirs, everything):
    columns = mine.shape[0]

    def kernel(own_ref, a_ref, b_ref, c_ref, d_ref, o_ref):
        own = own_ref[...] + times(b_ref[...], b_ref[...])
        cross = times(a_ref[...], c_ref[...]) + times(b_ref[...], d_ref[...])
        first = lax.axis_index("col") == 0
        both = jnp.concatenate([jnp.where(first, own, cross), jnp.where(first, cross, own)], axis=1)
        o_ref[...] = both * (1.0 / everything)

    return on_chip(kernel, (columns, 2 * columns), own, mine, theirs, other_mine, other_theirs)


def swap(value, k):
    return lax.ppermute(value, "row", [(i, i ^ step_of(k)) for i in range(lax.axis_size("row"))])


def body(matrix_panel, row_signs, sample_rows):
    devices = lax.axis_size("row")
    columns, _ = matrix_panel.shape
    everything = sample_rows.shape[0]
    bits = devices.bit_length() - 1

    def part(table, c0, c1):
        return pick(table, flat, rows, columns, corner_of(c0, c1))

    table, far, flat, rows = mix(matrix_panel, row_signs, sample_rows, devices, corner_of(1, 1))
    send = part(table, 0, 1) + swap(far, 0)
    table, send = lax.optimization_barrier((table, send))
    half = send.shape[0] // 2
    first = swap(send[half:], 1)
    second = swap(send[:half], 1)
    far = part(table, 1, 0)
    near = swap(far, 0)
    table, far = lax.optimization_barrier((table, far))
    rest = part(table, 0, 0)
    keep = rest + near
    for k in range(2, bits - 1):
        send = keep[half:] + first
        send, low = lax.optimization_barrier((send, keep[:half]))
        half = half // 2
        if k < bits - 2:
            first, later = swap(send[half:], k), swap(send[:half], k)
            keep = low + second
            second = later
        else:
            moved = swap(send, k)
            keep = low + second
    theirs = keep[1] + moved[1]
    mine = keep[0] + moved[0]
    theirs, mine = lax.optimization_barrier((theirs, mine))
    around = [(0, 1), (1, 0)]
    first = swap(theirs, bits - 1)
    second = swap(mine, bits - 1)
    mine = mine + first
    mine, theirs = lax.optimization_barrier((mine, theirs))
    theirs = theirs + second
    other_mine = lax.ppermute(mine, "col", around)
    own = square(mine)
    other_theirs = lax.ppermute(theirs, "col", around)
    gram = products(own, mine, theirs, other_mine, other_theirs, everything)
    for k in range(bits - 1):
        gram = gram + swap(gram, k)
    return (mine, gram)


def solution(mesh):
    return jax.shard_map(
        body,
        mesh=mesh,
        in_specs=(P("col", "row"), P("row"), P()),
        out_specs=(P("col", "row"), P("col", None)),
        check_vma=False,
    )
```

```python
import jax
import jax.numpy as jnp
import numpy as np
from jax import lax
from jax.experimental import pallas as pl
from jax.experimental.pallas import tpu as pltpu
from jax.sharding import PartitionSpec as P


WIDE = 256
LANES = 128
VMEM_GRANT = 16 << 20
CHUNKS = 1
SLOTS = 4


def in_space(value, space):
    return pltpu.with_memory_space_constraint(value, space)


def parity(value, bits):
    total = jnp.zeros_like(value)
    for k in range(bits):
        total = total ^ (value >> k)
    return total & 1


def mix_blocks(x_hbm, s_ref, s_copy, x_ref, t_ref, sems):
    _, length = x_ref.shape
    slabs = length // WIDE // 2
    groups = slabs // 2
    span = 2 * WIDE
    half = length // 2
    copies = []
    chunk = groups * span // CHUNKS
    for g in range(CHUNKS):
        for h in range(2):
            window = pl.ds(h * half + g * chunk, chunk)
            copies.append(pltpu.make_async_copy(x_hbm.at[:, window], x_ref.at[:, window], sems.at[g, h]))
            copies[-1].start()
    left = lax.broadcasted_iota(jnp.int32, (WIDE, WIDE), 0)
    right = lax.broadcasted_iota(jnp.int32, (WIDE, WIDE), 1)
    mat = (1 - 2 * parity(left & right, WIDE.bit_length() - 1)).astype(jnp.float32).astype(jnp.bfloat16)
    s_copy.wait()
    for g in range(groups):
        if g % (groups // CHUNKS) == 0:
            first = g // (groups // CHUNKS)
            copies[2 * first].wait()
            copies[2 * first + 1].wait()
        parts = []
        for q in range(2):
            for h in range(2):
                block = h * slabs + 2 * g + q
                signs = jnp.concatenate([s_ref[2 * block:2 * block + 1, :], s_ref[2 * block + 1:2 * block + 2, :]], axis=1)
                parts.append(x_ref[:, block * WIDE:(block + 1) * WIDE] * signs.astype(jnp.float32).astype(jnp.bfloat16))
        stacked = jnp.concatenate(parts, axis=0)
        out = lax.dot_general(mat, stacked, (((1,), (1,)), ((), ())), preferred_element_type=jnp.float32)
        one, two = out[:, :LANES], out[:, LANES:]
        t_ref[(2 * g) * WIDE:(2 * g + 1) * WIDE, :] = one + two
        t_ref[(2 * g + 1) * WIDE:(2 * g + 2) * WIDE, :] = one - two

    def butterfly(i, _):
        for q in range(2):
            at = [pl.ds(pl.multiple_of((2 * g + q) * WIDE + i * 8, 8), 8) for g in range(groups)]
            v = [t_ref[a, :] for a in at]
            step = 1
            while step < groups:
                for j in range(groups):
                    if not j & step:
                        v[j], v[j + step] = v[j] + v[j + step], v[j] - v[j + step]
                step *= 2
            for a, value in zip(at, v):
                t_ref[a, :] = value
        return 0

    lax.fori_loop(0, WIDE // 8, butterfly, 0, unroll=4)


def step_of(k, odd):
    straight, crossed = (1 << k) | 1, (1 << {1: 2, 2: 1}.get(k, k)) | 1
    if isinstance(odd, int):
        return crossed if odd else straight
    return straight + odd * (crossed - straight)


def gather_blocks(devices, length, columns, corner, rows_smem, rows_ref, t_ref, g_ref, out_ref):
    per = rows_ref.shape[1]
    half = length // 2
    bits = devices.bit_length() - 1
    top = length.bit_length() - 2
    scale = float(1.0 / np.sqrt(float(length) * devices))
    me = lax.axis_index("row")
    c0, c1 = corner
    odd = c0
    for k in range(bits):
        odd = odd ^ ((me >> k) & 1)
    origin = me ^ c0 ^ (c1 * step_of(1, odd))

    def gather(i, slot):
        dest = origin
        for k in range(2, bits):
            dest = dest ^ (((i >> (bits - 1 - k)) & 1) * step_of(k, odd))
        for t in range(per):
            row = rows_smem[dest * per + t] & (half - 1)
            g_ref[slot][t:t + 1, :] = t_ref[pl.ds(row, 1), :]
        turned = g_ref[slot][...].T
        samples = rows_ref[pl.ds(dest, 1), :]
        flip = parity((samples >> (top + 1)) & me, bits)
        first = jnp.where(flip == 1, -scale, scale)
        second = jnp.where((flip ^ ((samples >> top) & 1)) == 1, -scale, scale)
        out_ref[i] = turned[:columns, :] * first + turned[columns:, :] * second

    def several(j, _):
        for slot in range(SLOTS):
            gather(j * SLOTS + slot, slot)
        return 0

    lax.fori_loop(0, out_ref.shape[0] // SLOTS, several, 0)


def mix(matrix_panel, row_signs, sample_rows, devices, corner):
    columns, length = matrix_panel.shape
    per = sample_rows.shape[0] // devices
    hbm, vmem, smem = (pl.BlockSpec(memory_space=m) for m in (pltpu.HBM, pltpu.VMEM, pltpu.SMEM))

    def kernel(x_hbm, s_hbm, flat_hbm, rows_hbm, t_ref, out_ref, flat_ref, rows_ref, x_ref, s_ref, *rest):
        g_ref, (sems, more) = rest[:SLOTS], rest[SLOTS:]
        fetch = [pltpu.make_async_copy(a, b, more.at[k]) for k, (a, b) in enumerate(((s_hbm, s_ref), (flat_hbm, flat_ref), (rows_hbm, rows_ref)))]
        for copy in fetch:
            copy.start()
        mix_blocks(x_hbm, s_ref, fetch[0], x_ref, t_ref, sems)
        fetch[1].wait()
        fetch[2].wait()
        gather_blocks(devices, length, columns, corner, flat_ref, rows_ref, t_ref, g_ref, out_ref)

    return pl.pallas_call(
        kernel,
        out_shape=(
            pltpu.VMEM((length // 2, LANES), jnp.float32),
            pltpu.VMEM((devices // 4, columns, per), jnp.float32),
            pltpu.SMEM(sample_rows.shape, jnp.int32),
            pltpu.VMEM((devices, per), jnp.int32),
        ),
        in_specs=[hbm] * 4,
        out_specs=(vmem, vmem, smem, vmem),
        scratch_shapes=[
            pltpu.VMEM((columns, length), jnp.bfloat16),
            pltpu.VMEM((length // LANES, LANES), jnp.int32),
            *[pltpu.VMEM((per, LANES), jnp.float32)] * SLOTS,
            pltpu.SemaphoreType.DMA((CHUNKS, 2)),
            pltpu.SemaphoreType.DMA((3,)),
        ],
        compiler_params=pltpu.CompilerParams(vmem_limit_bytes=VMEM_GRANT),
    )(*(in_space(a, pltpu.HBM) for a in (matrix_panel, row_signs.reshape(length // LANES, LANES), sample_rows, sample_rows.reshape(devices, per))))


def pick(table, flat, rows, columns, corner):
    devices, per = rows.shape
    vmem, smem = pl.BlockSpec(memory_space=pltpu.VMEM), pl.BlockSpec(memory_space=pltpu.SMEM)
    length = 2 * table.shape[0]

    def kernel(t_ref, flat_ref, rows_ref, out_ref, *g_ref):
        gather_blocks(devices, length, columns, corner, flat_ref, rows_ref, t_ref, g_ref, out_ref)

    return pl.pallas_call(
        kernel,
        out_shape=pltpu.VMEM((devices // 4, columns, per), jnp.float32),
        in_specs=[vmem, smem, vmem],
        scratch_shapes=[pltpu.VMEM((per, LANES), jnp.float32)] * SLOTS,
        compiler_params=pltpu.CompilerParams(vmem_limit_bytes=VMEM_GRANT),
    )(in_space(table, pltpu.VMEM), in_space(flat, pltpu.SMEM), in_space(rows, pltpu.VMEM))


def times(left, right):
    return lax.dot_general(left, right, (((1,), (1,)), ((), ())), precision=lax.Precision.HIGHEST)


def on_chip(kernel, shape, *operands):
    return pl.pallas_call(
        kernel,
        out_shape=pltpu.VMEM(shape, jnp.float32),
        in_specs=[pl.BlockSpec(memory_space=pltpu.VMEM)] * len(operands),
        compiler_params=pltpu.CompilerParams(vmem_limit_bytes=VMEM_GRANT),
    )(*(in_space(a, pltpu.VMEM) for a in operands))


def products(full, other, everything):
    blocks, columns, _ = full.shape

    def kernel(a_ref, b_ref, o_ref):
        own = sum(times(a_ref[i], a_ref[i]) for i in range(blocks))
        cross = sum(times(a_ref[i], b_ref[i]) for i in range(blocks))
        first = lax.axis_index("col") == 0
        both = jnp.concatenate([jnp.where(first, own, cross), jnp.where(first, cross, own)], axis=1)
        o_ref[...] = both * (1.0 / everything)

    return on_chip(kernel, (columns, 2 * columns), full, other)


def swap(value, k):
    size = lax.axis_size("row")
    return lax.ppermute(value, "row", [(i, i ^ (step_of(k, i.bit_count() & 1) if k else 1)) for i in range(size)])


def body(matrix_panel, row_signs, sample_rows):
    devices = lax.axis_size("row")
    columns, _ = matrix_panel.shape
    everything = sample_rows.shape[0]
    bits = devices.bit_length() - 1

    def part(table, c0, c1):
        return pick(table, flat, rows, columns, (c0, c1))

    table, far, flat, rows = mix(matrix_panel, row_signs, sample_rows, devices, (1, 1))
    send = part(table, 0, 1) + swap(far, 0)
    table, send = lax.optimization_barrier((table, send))
    half = send.shape[0] // 2
    first = swap(send[half:], 1)
    second = swap(send[:half], 1)
    far = part(table, 1, 0)
    near = swap(far, 0)
    table, far = lax.optimization_barrier((table, far))
    rest = part(table, 0, 0)
    keep = rest + near
    for k in range(2, bits - 1):
        send = keep[half:] + first
        send, low = lax.optimization_barrier((send, keep[:half]))
        half = half // 2
        if k < bits - 2:
            first, later = swap(send[half:], k), swap(send[:half], k)
            keep = low + second
            second = later
        else:
            moved = swap(send, k)
            keep = low + second
    total = keep + moved
    moved = swap(total, bits - 1)
    mine = total[0] + moved[1]
    theirs = total[1] + moved[0]
    full = jnp.concatenate([mine[None], theirs[None]], axis=0)
    other = lax.ppermute(full, "col", [(0, 1), (1, 0)])
    gram = products(full, other, everything)
    for k in range(bits - 1):
        gram = gram + swap(gram, k)
    return (mine, gram)


def solution(mesh):
    return jax.shard_map(
        body,
        mesh=mesh,
        in_specs=(P("col", "row"), P("row"), P()),
        out_specs=(P("col", "row"), P("col", None)),
        check_vma=False,
    )
```

```python
import jax
import jax.numpy as jnp
import numpy as np
from jax import lax
from jax.experimental import pallas as pl
from jax.experimental.pallas import tpu as pltpu
from jax.sharding import PartitionSpec as P


WIDE = 256
LANES = 128
VMEM_GRANT = 16 << 20
CHUNKS = 1
SLOTS = 4


def in_space(value, space):
    return pltpu.with_memory_space_constraint(value, space)


def parity(value, bits):
    total = jnp.zeros_like(value)
    for k in range(bits):
        total = total ^ (value >> k)
    return total & 1


def mix_blocks(x_hbm, s_ref, s_copy, x_ref, t_ref, sems):
    _, length = x_ref.shape
    slabs = length // WIDE // 2
    groups = slabs // 2
    span = 2 * WIDE
    half = length // 2
    copies = []
    chunk = groups * span // CHUNKS
    for g in range(CHUNKS):
        for h in range(2):
            window = pl.ds(h * half + g * chunk, chunk)
            copies.append(pltpu.make_async_copy(x_hbm.at[:, window], x_ref.at[:, window], sems.at[g, h]))
            copies[-1].start()
    left = lax.broadcasted_iota(jnp.int32, (WIDE, WIDE), 0)
    right = lax.broadcasted_iota(jnp.int32, (WIDE, WIDE), 1)
    mat = (1 - 2 * parity(left & right, WIDE.bit_length() - 1)).astype(jnp.float32).astype(jnp.bfloat16)
    s_copy.wait()
    for g in range(groups):
        if g % (groups // CHUNKS) == 0:
            first = g // (groups // CHUNKS)
            copies[2 * first].wait()
            copies[2 * first + 1].wait()
        parts = []
        for q in range(2):
            for h in range(2):
                block = h * slabs + 2 * g + q
                signs = jnp.concatenate([s_ref[2 * block:2 * block + 1, :], s_ref[2 * block + 1:2 * block + 2, :]], axis=1)
                parts.append(x_ref[:, block * WIDE:(block + 1) * WIDE] * signs.astype(jnp.float32).astype(jnp.bfloat16))
        stacked = jnp.concatenate(parts, axis=0)
        out = lax.dot_general(mat, stacked, (((1,), (1,)), ((), ())), preferred_element_type=jnp.float32)
        one, two = out[:, :LANES], out[:, LANES:]
        t_ref[(2 * g) * WIDE:(2 * g + 1) * WIDE, :] = one + two
        t_ref[(2 * g + 1) * WIDE:(2 * g + 2) * WIDE, :] = one - two

    def butterfly(i, _):
        for q in range(2):
            at = [pl.ds(pl.multiple_of((2 * g + q) * WIDE + i * 8, 8), 8) for g in range(groups)]
            v = [t_ref[a, :] for a in at]
            step = 1
            while step < groups:
                for j in range(groups):
                    if not j & step:
                        v[j], v[j + step] = v[j] + v[j + step], v[j] - v[j + step]
                step *= 2
            for a, value in zip(at, v):
                t_ref[a, :] = value
        return 0

    lax.fori_loop(0, WIDE // 8, butterfly, 0, unroll=4)


def step_of(k, odd):
    straight, crossed = (1 << k) | 1, (1 << {1: 2, 2: 1}.get(k, k)) | 1
    if isinstance(odd, int):
        return crossed if odd else straight
    return straight + odd * (crossed - straight)


def gather_blocks(devices, length, columns, corner, rows_smem, rows_ref, t_ref, g_ref, out_ref):
    per = rows_ref.shape[1]
    half = length // 2
    bits = devices.bit_length() - 1
    top = length.bit_length() - 2
    scale = float(1.0 / np.sqrt(float(length) * devices))
    me = lax.axis_index("row")
    c0, c1 = corner
    odd = c0
    for k in range(bits):
        odd = odd ^ ((me >> k) & 1)
    origin = me ^ (lax.axis_index("col") & 1) ^ c0 ^ (c1 * step_of(1, odd))

    def gather(i, slot):
        dest = origin
        for k in range(2, bits):
            dest = dest ^ (((i >> (bits - 1 - k)) & 1) * step_of(k, odd))
        for t in range(per):
            row = rows_smem[dest * per + t] & (half - 1)
            g_ref[slot][t:t + 1, :] = t_ref[pl.ds(row, 1), :]
        turned = g_ref[slot][...].T
        samples = rows_ref[pl.ds(dest, 1), :]
        flip = parity((samples >> (top + 1)) & me, bits)
        first = jnp.where(flip == 1, -scale, scale)
        second = jnp.where((flip ^ ((samples >> top) & 1)) == 1, -scale, scale)
        out_ref[i] = turned[:columns, :] * first + turned[columns:, :] * second

    def several(j, _):
        for slot in range(SLOTS):
            gather(j * SLOTS + slot, slot)
        return 0

    lax.fori_loop(0, out_ref.shape[0] // SLOTS, several, 0)


def mix(matrix_panel, row_signs, sample_rows, devices, corner):
    columns, length = matrix_panel.shape
    per = sample_rows.shape[0] // devices
    hbm, vmem, smem = (pl.BlockSpec(memory_space=m) for m in (pltpu.HBM, pltpu.VMEM, pltpu.SMEM))

    def kernel(x_hbm, s_hbm, flat_hbm, rows_hbm, t_ref, out_ref, flat_ref, rows_ref, x_ref, s_ref, *rest):
        g_ref, (sems, more) = rest[:SLOTS], rest[SLOTS:]
        fetch = [pltpu.make_async_copy(a, b, more.at[k]) for k, (a, b) in enumerate(((s_hbm, s_ref), (flat_hbm, flat_ref), (rows_hbm, rows_ref)))]
        for copy in fetch:
            copy.start()
        mix_blocks(x_hbm, s_ref, fetch[0], x_ref, t_ref, sems)
        fetch[1].wait()
        fetch[2].wait()
        gather_blocks(devices, length, columns, corner, flat_ref, rows_ref, t_ref, g_ref, out_ref)

    return pl.pallas_call(
        kernel,
        out_shape=(
            pltpu.VMEM((length // 2, LANES), jnp.float32),
            pltpu.VMEM((devices // 4, columns, per), jnp.float32),
            pltpu.SMEM(sample_rows.shape, jnp.int32),
            pltpu.VMEM((devices, per), jnp.int32),
        ),
        in_specs=[hbm] * 4,
        out_specs=(vmem, vmem, smem, vmem),
        scratch_shapes=[
            pltpu.VMEM((columns, length), jnp.bfloat16),
            pltpu.VMEM((length // LANES, LANES), jnp.int32),
            *[pltpu.VMEM((per, LANES), jnp.float32)] * SLOTS,
            pltpu.SemaphoreType.DMA((CHUNKS, 2)),
            pltpu.SemaphoreType.DMA((3,)),
        ],
        compiler_params=pltpu.CompilerParams(vmem_limit_bytes=VMEM_GRANT),
    )(*(in_space(a, pltpu.HBM) for a in (matrix_panel, row_signs.reshape(length // LANES, LANES), sample_rows, sample_rows.reshape(devices, per))))


def pick(table, flat, rows, columns, corner):
    devices, per = rows.shape
    vmem, smem = pl.BlockSpec(memory_space=pltpu.VMEM), pl.BlockSpec(memory_space=pltpu.SMEM)
    length = 2 * table.shape[0]

    def kernel(t_ref, flat_ref, rows_ref, out_ref, *g_ref):
        gather_blocks(devices, length, columns, corner, flat_ref, rows_ref, t_ref, g_ref, out_ref)

    return pl.pallas_call(
        kernel,
        out_shape=pltpu.VMEM((devices // 4, columns, per), jnp.float32),
        in_specs=[vmem, smem, vmem],
        scratch_shapes=[pltpu.VMEM((per, LANES), jnp.float32)] * SLOTS,
        compiler_params=pltpu.CompilerParams(vmem_limit_bytes=VMEM_GRANT),
    )(in_space(table, pltpu.VMEM), in_space(flat, pltpu.SMEM), in_space(rows, pltpu.VMEM))


def times(left, right):
    return lax.dot_general(left, right, (((1,), (1,)), ((), ())), precision=lax.Precision.HIGHEST)


def on_chip(kernel, shape, *operands):
    return pl.pallas_call(
        kernel,
        out_shape=pltpu.VMEM(shape, jnp.float32),
        in_specs=[pl.BlockSpec(memory_space=pltpu.VMEM)] * len(operands),
        compiler_params=pltpu.CompilerParams(vmem_limit_bytes=VMEM_GRANT),
    )(*(in_space(a, pltpu.VMEM) for a in operands))


def square(full):
    blocks, columns, _ = full.shape

    def kernel(a_ref, o_ref):
        o_ref[...] = sum(times(a_ref[i], a_ref[i]) for i in range(blocks))

    return on_chip(kernel, (columns, columns), full)


def products(own, full, other, everything):
    blocks, columns, _ = full.shape

    def kernel(own_ref, a_ref, b_ref, o_ref):
        own = own_ref[...]
        cross = sum(times(a_ref[i], b_ref[i]) for i in range(blocks))
        first = lax.axis_index("col") == 0
        both = jnp.concatenate([jnp.where(first, own, cross), jnp.where(first, cross, own)], axis=1)
        o_ref[...] = both * (1.0 / everything)

    return on_chip(kernel, (columns, 2 * columns), own, full, other)


def choose(mine, traded):
    def kernel(a_ref, b_ref, o_ref):
        o_ref[...] = jnp.where(lax.axis_index("col") & 1 == 0, a_ref[...], b_ref[...])

    return on_chip(kernel, mine.shape, mine, traded)


def swap(value, k):
    size = lax.axis_size("row")
    return lax.ppermute(value, "row", [(i, i ^ (step_of(k, i.bit_count() & 1) if k else 1)) for i in range(size)])


def body(matrix_panel, row_signs, sample_rows):
    devices = lax.axis_size("row")
    columns, _ = matrix_panel.shape
    everything = sample_rows.shape[0]
    bits = devices.bit_length() - 1

    def part(table, c0, c1):
        return pick(table, flat, rows, columns, (c0, c1))

    table, far, flat, rows = mix(matrix_panel, row_signs, sample_rows, devices, (1, 1))
    send = part(table, 0, 1) + swap(far, 0)
    table, send = lax.optimization_barrier((table, send))
    half = send.shape[0] // 2
    first = swap(send[half:], 1)
    second = swap(send[:half], 1)
    far = part(table, 1, 0)
    near = swap(far, 0)
    table, far = lax.optimization_barrier((table, far))
    rest = part(table, 0, 0)
    keep = rest + near
    for k in range(2, bits - 1):
        send = keep[half:] + first
        send, low = lax.optimization_barrier((send, keep[:half]))
        half = half // 2
        if k < bits - 2:
            first, later = swap(send[half:], k), swap(send[:half], k)
            keep = low + second
            second = later
        else:
            moved = swap(send, k)
            keep = low + second
    total = keep + moved
    moved = swap(total, bits - 1)
    mine = total[0] + moved[1]
    theirs = total[1] + moved[0]
    full = jnp.concatenate([mine[None], theirs[None]], axis=0)
    size = lax.axis_size("col")
    around = [(r * size + c, (r ^ 1) * size + (c ^ 1)) for r in range(devices) for c in range(size)]
    other = lax.ppermute(full, ("row", "col"), around)
    traded = swap(mine, 0)
    own = square(full)
    gram = products(own, full, other, everything)
    for k in range(bits - 1):
        gram = gram + swap(gram, k)
    sketch = choose(mine, traded)
    return (sketch, gram)


def solution(mesh):
    return jax.shard_map(
        body,
        mesh=mesh,
        in_specs=(P("col", "row"), P("row"), P()),
        out_specs=(P("col", "row"), P("col", None)),
        check_vma=False,
    )
```

```python
import jax
import jax.numpy as jnp
import numpy as np
from jax import lax
from jax.experimental import pallas as pl
from jax.experimental.pallas import tpu as pltpu
from jax.sharding import PartitionSpec as P


WIDE = 256
LANES = 128
VMEM_GRANT = 16 << 20
CHUNKS = 1
SLOTS = 4


def in_space(value, space):
    return pltpu.with_memory_space_constraint(value, space)


def parity(value, bits):
    total = jnp.zeros_like(value)
    for k in range(bits):
        total = total ^ (value >> k)
    return total & 1


def mix_blocks(x_hbm, s_ref, ready, x_ref, t_ref, sems):
    _, length = x_ref.shape
    slabs = length // WIDE // 2
    groups = slabs // 2
    span = 2 * WIDE
    half = length // 2
    copies = []
    chunk = groups * span // CHUNKS
    for g in range(CHUNKS):
        for h in range(2):
            window = pl.ds(h * half + g * chunk, chunk)
            copies.append(pltpu.make_async_copy(x_hbm.at[:, window], x_ref.at[:, window], sems.at[g, h]))
            copies[-1].start()
    left = lax.broadcasted_iota(jnp.int32, (WIDE, WIDE), 0)
    right = lax.broadcasted_iota(jnp.int32, (WIDE, WIDE), 1)
    mat = (1 - 2 * parity(left & right, WIDE.bit_length() - 1)).astype(jnp.float32).astype(jnp.bfloat16)
    ready()
    for g in range(groups):
        if g % (groups // CHUNKS) == 0:
            first = g // (groups // CHUNKS)
            copies[2 * first].wait()
            copies[2 * first + 1].wait()
        parts = []
        for q in range(2):
            for h in range(2):
                block = h * slabs + 2 * g + q
                signs = jnp.concatenate([s_ref[2 * block:2 * block + 1, :], s_ref[2 * block + 1:2 * block + 2, :]], axis=1)
                parts.append(x_ref[:, block * WIDE:(block + 1) * WIDE] * signs.astype(jnp.float32).astype(jnp.bfloat16))
        stacked = jnp.concatenate(parts, axis=0)
        out = lax.dot_general(mat, stacked, (((1,), (1,)), ((), ())), preferred_element_type=jnp.float32)
        one, two = out[:, :LANES], out[:, LANES:]
        t_ref[(2 * g) * WIDE:(2 * g + 1) * WIDE, :] = one + two
        t_ref[(2 * g + 1) * WIDE:(2 * g + 2) * WIDE, :] = one - two

    def butterfly(i, _):
        for q in range(2):
            at = [pl.ds(pl.multiple_of((2 * g + q) * WIDE + i * 8, 8), 8) for g in range(groups)]
            v = [t_ref[a, :] for a in at]
            step = 1
            while step < groups:
                for j in range(groups):
                    if not j & step:
                        v[j], v[j + step] = v[j] + v[j + step], v[j] - v[j + step]
                step *= 2
            for a, value in zip(at, v):
                t_ref[a, :] = value
        return 0

    lax.fori_loop(0, WIDE // 8, butterfly, 0, unroll=4)


def step_of(k, odd):
    straight, crossed = (1 << k) | 1, (1 << {1: 2, 2: 1}.get(k, k)) | 1
    if isinstance(odd, int):
        return crossed if odd else straight
    return straight + odd * (crossed - straight)


def gather_blocks(devices, length, columns, corner, rows_smem, rows_ref, t_ref, out_ref):
    per = rows_ref.shape[1]
    bits = devices.bit_length() - 1
    top = length.bit_length() - 2
    scale = float(1.0 / np.sqrt(float(length) * devices))
    me = lax.axis_index("row")
    c0, c1 = corner
    odd = c0
    for k in range(bits):
        odd = odd ^ ((me >> k) & 1)
    origin = me ^ (lax.axis_index("col") & 1) ^ c0 ^ (c1 * step_of(1, odd))

    def gather(i):
        dest = origin
        for k in range(2, bits):
            dest = dest ^ (((i >> (bits - 1 - k)) & 1) * step_of(k, odd))
        turned = jnp.concatenate([t_ref[pl.ds(rows_smem[dest, t], 1), :] for t in range(per)], axis=0).T
        samples = rows_ref[pl.ds(dest, 1), :]
        flip = parity((samples >> (top + 1)) & me, bits)
        first = jnp.where(flip == 1, -scale, scale)
        second = jnp.where((flip ^ ((samples >> top) & 1)) == 1, -scale, scale)
        out_ref[i] = turned[:columns, :] * first + turned[columns:, :] * second

    def several(j, _):
        for slot in range(SLOTS):
            gather(j * SLOTS + slot)
        return 0

    lax.fori_loop(0, out_ref.shape[0] // SLOTS, several, 0)


def mix(matrix_panel, row_signs, sample_rows, devices, corner):
    columns, length = matrix_panel.shape
    per = sample_rows.shape[0] // devices
    hbm, vmem, smem = (pl.BlockSpec(memory_space=m) for m in (pltpu.HBM, pltpu.VMEM, pltpu.SMEM))

    def kernel(x_hbm, s_hbm, rows_hbm, t_ref, out_ref, flat_ref, rows_ref, x_ref, s_ref, masked_ref, sems, more):
        fetch = [pltpu.make_async_copy(a, b, more.at[k]) for k, (a, b) in enumerate(((s_hbm, s_ref), (rows_hbm, rows_ref)))]
        for copy in fetch:
            copy.start()
        move = pltpu.make_async_copy(masked_ref, flat_ref, more.at[2])

        def ready():
            fetch[1].wait()
            masked_ref[...] = rows_ref[...] & (length // 2 - 1)
            move.start()
            fetch[0].wait()

        mix_blocks(x_hbm, s_ref, ready, x_ref, t_ref, sems)
        move.wait()
        gather_blocks(devices, length, columns, corner, flat_ref, rows_ref, t_ref, out_ref)

    return pl.pallas_call(
        kernel,
        out_shape=(
            pltpu.VMEM((length // 2, LANES), jnp.float32),
            pltpu.VMEM((devices // 4, columns, per), jnp.float32),
            pltpu.SMEM((devices, per), jnp.int32),
            pltpu.VMEM((devices, per), jnp.int32),
        ),
        in_specs=[hbm] * 3,
        out_specs=(vmem, vmem, smem, vmem),
        scratch_shapes=[
            pltpu.VMEM((columns, length), jnp.bfloat16),
            pltpu.VMEM((length // LANES, LANES), jnp.int32),
            pltpu.VMEM((devices, per), jnp.int32),
            pltpu.SemaphoreType.DMA((CHUNKS, 2)),
            pltpu.SemaphoreType.DMA((3,)),
        ],
        compiler_params=pltpu.CompilerParams(vmem_limit_bytes=VMEM_GRANT),
    )(*(in_space(a, pltpu.HBM) for a in (matrix_panel, row_signs.reshape(length // LANES, LANES), sample_rows.reshape(devices, per))))


def pick(table, flat, rows, columns, corner):
    devices, per = rows.shape
    vmem, smem = pl.BlockSpec(memory_space=pltpu.VMEM), pl.BlockSpec(memory_space=pltpu.SMEM)
    length = 2 * table.shape[0]

    def kernel(t_ref, flat_ref, rows_ref, out_ref):
        gather_blocks(devices, length, columns, corner, flat_ref, rows_ref, t_ref, out_ref)

    return pl.pallas_call(
        kernel,
        out_shape=pltpu.VMEM((devices // 4, columns, per), jnp.float32),
        in_specs=[vmem, smem, vmem],
        compiler_params=pltpu.CompilerParams(vmem_limit_bytes=VMEM_GRANT),
    )(in_space(table, pltpu.VMEM), in_space(flat, pltpu.SMEM), in_space(rows, pltpu.VMEM))


def times(left, right):
    return lax.dot_general(left, right, (((1,), (1,)), ((), ())), precision=lax.Precision.HIGHEST)


def on_chip(kernel, shape, *operands):
    return pl.pallas_call(
        kernel,
        out_shape=pltpu.VMEM(shape, jnp.float32),
        in_specs=[pl.BlockSpec(memory_space=pltpu.VMEM)] * len(operands),
        compiler_params=pltpu.CompilerParams(vmem_limit_bytes=VMEM_GRANT),
    )(*(in_space(a, pltpu.VMEM) for a in operands))


def square(full):
    blocks, columns, _ = full.shape

    def kernel(a_ref, o_ref):
        o_ref[...] = sum(times(a_ref[i], a_ref[i]) for i in range(blocks))

    return on_chip(kernel, (columns, columns), full)


def products(own, full, other, everything):
    blocks, columns, _ = full.shape

    def kernel(own_ref, a_ref, b_ref, o_ref):
        own = own_ref[...]
        cross = sum(times(a_ref[i], b_ref[i]) for i in range(blocks))
        first = lax.axis_index("col") == 0
        both = jnp.concatenate([jnp.where(first, own, cross), jnp.where(first, cross, own)], axis=1)
        o_ref[...] = both * (1.0 / everything)

    return on_chip(kernel, (columns, 2 * columns), own, full, other)


def choose(mine, traded):
    def kernel(a_ref, b_ref, o_ref):
        o_ref[...] = jnp.where(lax.axis_index("col") & 1 == 0, a_ref[...], b_ref[...])

    return on_chip(kernel, mine.shape, mine, traded)


def swap(value, k):
    size = lax.axis_size("row")
    return lax.ppermute(value, "row", [(i, i ^ (step_of(k, i.bit_count() & 1) if k else 1)) for i in range(size)])


def body(matrix_panel, row_signs, sample_rows):
    devices = lax.axis_size("row")
    columns, _ = matrix_panel.shape
    everything = sample_rows.shape[0]
    bits = devices.bit_length() - 1

    def part(table, c0, c1):
        return pick(table, flat, rows, columns, (c0, c1))

    table, far, flat, rows = mix(matrix_panel, row_signs, sample_rows, devices, (1, 1))
    send = part(table, 0, 1) + swap(far, 0)
    table, send = lax.optimization_barrier((table, send))
    half = send.shape[0] // 2
    first = swap(send[half:], 1)
    second = swap(send[:half], 1)
    far = part(table, 1, 0)
    near = swap(far, 0)
    table, far = lax.optimization_barrier((table, far))
    rest = part(table, 0, 0)
    keep = rest + near
    for k in range(2, bits - 1):
        send = keep[half:] + first
        send, low = lax.optimization_barrier((send, keep[:half]))
        half = half // 2
        if k < bits - 2:
            first, later = swap(send[half:], k), swap(send[:half], k)
            keep = low + second
            second = later
        else:
            moved = swap(send, k)
            keep = low + second
    total = keep + moved
    moved = swap(total, bits - 1)
    mine = total[0] + moved[1]
    theirs = total[1] + moved[0]
    full = jnp.concatenate([mine[None], theirs[None]], axis=0)
    size = lax.axis_size("col")
    around = [(r * size + c, (r ^ 1) * size + (c ^ 1)) for r in range(devices) for c in range(size)]
    other = lax.ppermute(full, ("row", "col"), around)
    traded = swap(mine, 0)
    own = square(full)
    gram = products(own, full, other, everything)
    for k in range(bits - 1):
        gram = gram + swap(gram, k)
    sketch = choose(mine, traded)
    return (sketch, gram)


def solution(mesh):
    return jax.shard_map(
        body,
        mesh=mesh,
        in_specs=(P("col", "row"), P("row"), P()),
        out_specs=(P("col", "row"), P("col", None)),
        check_vma=False,
    )
```

```python
import jax
import jax.numpy as jnp
import numpy as np
from jax import lax
from jax.experimental import pallas as pl
from jax.experimental.pallas import tpu as pltpu
from jax.sharding import PartitionSpec as P


WIDE = 256
LANES = 128
VMEM_GRANT = 16 << 20
CHUNKS = 1
SLOTS = 4


def in_space(value, space):
    return pltpu.with_memory_space_constraint(value, space)


def parity(value, bits):
    total = jnp.zeros_like(value)
    for k in range(bits):
        total = total ^ (value >> k)
    return total & 1


def mix_blocks(x_hbm, s_ref, ready, x_ref, t_ref, sems):
    _, length = x_ref.shape
    slabs = length // WIDE // 2
    groups = slabs // 2
    span = 2 * WIDE
    half = length // 2
    copies = []
    chunk = groups * span // CHUNKS
    for g in range(CHUNKS):
        for h in range(2):
            window = pl.ds(h * half + g * chunk, chunk)
            copies.append(pltpu.make_async_copy(x_hbm.at[:, window], x_ref.at[:, window], sems.at[g, h]))
            copies[-1].start()
    left = lax.broadcasted_iota(jnp.int32, (WIDE, WIDE), 0)
    right = lax.broadcasted_iota(jnp.int32, (WIDE, WIDE), 1)
    mat = (1 - 2 * parity(left & right, WIDE.bit_length() - 1)).astype(jnp.float32).astype(jnp.bfloat16)
    ready()
    for g in range(groups):
        if g % (groups // CHUNKS) == 0:
            first = g // (groups // CHUNKS)
            copies[2 * first].wait()
            copies[2 * first + 1].wait()
        parts = []
        for q in range(2):
            for h in range(2):
                block = h * slabs + 2 * g + q
                signs = jnp.concatenate([s_ref[2 * block:2 * block + 1, :], s_ref[2 * block + 1:2 * block + 2, :]], axis=1)
                parts.append(x_ref[:, block * WIDE:(block + 1) * WIDE] * signs.astype(jnp.float32).astype(jnp.bfloat16))
        stacked = jnp.concatenate(parts, axis=0)
        out = lax.dot_general(mat, stacked, (((1,), (1,)), ((), ())), preferred_element_type=jnp.float32)
        one, two = out[:, :LANES], out[:, LANES:]
        t_ref[(2 * g) * WIDE:(2 * g + 1) * WIDE, :] = one + two
        t_ref[(2 * g + 1) * WIDE:(2 * g + 2) * WIDE, :] = one - two

    def butterfly(i, _):
        for q in range(2):
            at = [pl.ds(pl.multiple_of((2 * g + q) * WIDE + i * 8, 8), 8) for g in range(groups)]
            v = [t_ref[a, :] for a in at]
            step = 1
            while step < groups:
                for j in range(groups):
                    if not j & step:
                        v[j], v[j + step] = v[j] + v[j + step], v[j] - v[j + step]
                step *= 2
            for a, value in zip(at, v):
                t_ref[a, :] = value
        return 0

    lax.fori_loop(0, WIDE // 8, butterfly, 0, unroll=16)


def step_of(k, odd):
    straight, crossed = (1 << k) | 1, (1 << {1: 2, 2: 1}.get(k, k)) | 1
    if isinstance(odd, int):
        return crossed if odd else straight
    return straight + odd * (crossed - straight)


def gather_blocks(devices, length, columns, corner, rows_smem, rows_ref, t_ref, out_ref):
    per = rows_ref.shape[1]
    bits = devices.bit_length() - 1
    top = length.bit_length() - 2
    scale = float(1.0 / np.sqrt(float(length) * devices))
    me = lax.axis_index("row")
    c0, c1 = corner
    odd = c0
    for k in range(bits):
        odd = odd ^ ((me >> k) & 1)
    origin = me ^ c0 ^ (c1 * step_of(1, odd))

    def gather(i):
        dest = origin
        for k in range(2, bits):
            dest = dest ^ (((i >> (bits - 1 - k)) & 1) * step_of(k, odd))
        turned = jnp.concatenate([t_ref[pl.ds(rows_smem[dest, t], 1), :] for t in range(per)], axis=0).T
        samples = rows_ref[pl.ds(dest, 1), :]
        flip = parity((samples >> (top + 1)) & me, bits)
        first = jnp.where(flip == 1, -scale, scale)
        second = jnp.where((flip ^ ((samples >> top) & 1)) == 1, -scale, scale)
        out_ref[i] = turned[:columns, :] * first + turned[columns:, :] * second

    def several(j, _):
        for slot in range(SLOTS):
            gather(j * SLOTS + slot)
        return 0

    lax.fori_loop(0, out_ref.shape[0] // SLOTS, several, 0)


def mix(matrix_panel, row_signs, sample_rows, devices, corner):
    columns, length = matrix_panel.shape
    per = sample_rows.shape[0] // devices
    hbm, vmem, smem = (pl.BlockSpec(memory_space=m) for m in (pltpu.HBM, pltpu.VMEM, pltpu.SMEM))

    def kernel(x_hbm, s_hbm, rows_hbm, t_ref, out_ref, flat_ref, rows_ref, x_ref, s_ref, masked_ref, sems, more):
        fetch = [pltpu.make_async_copy(a, b, more.at[k]) for k, (a, b) in enumerate(((s_hbm, s_ref), (rows_hbm, rows_ref)))]
        for copy in fetch:
            copy.start()
        move = pltpu.make_async_copy(masked_ref, flat_ref, more.at[2])

        def ready():
            fetch[1].wait()
            masked_ref[...] = rows_ref[...] & (length // 2 - 1)
            move.start()
            fetch[0].wait()

        mix_blocks(x_hbm, s_ref, ready, x_ref, t_ref, sems)
        move.wait()
        gather_blocks(devices, length, columns, corner, flat_ref, rows_ref, t_ref, out_ref)

    return pl.pallas_call(
        kernel,
        out_shape=(
            pltpu.VMEM((length // 2, LANES), jnp.float32),
            pltpu.VMEM((devices // 4, columns, per), jnp.float32),
            pltpu.SMEM((devices, per), jnp.int32),
            pltpu.VMEM((devices, per), jnp.int32),
        ),
        in_specs=[hbm] * 3,
        out_specs=(vmem, vmem, smem, vmem),
        scratch_shapes=[
            pltpu.VMEM((columns, length), jnp.bfloat16),
            pltpu.VMEM((length // LANES, LANES), jnp.int32),
            pltpu.VMEM((devices, per), jnp.int32),
            pltpu.SemaphoreType.DMA((CHUNKS, 2)),
            pltpu.SemaphoreType.DMA((3,)),
        ],
        compiler_params=pltpu.CompilerParams(vmem_limit_bytes=VMEM_GRANT),
    )(*(in_space(a, pltpu.HBM) for a in (matrix_panel, row_signs.reshape(length // LANES, LANES), sample_rows.reshape(devices, per))))


def pick(table, flat, rows, columns, corner):
    devices, per = rows.shape
    vmem, smem = pl.BlockSpec(memory_space=pltpu.VMEM), pl.BlockSpec(memory_space=pltpu.SMEM)
    length = 2 * table.shape[0]

    def kernel(t_ref, flat_ref, rows_ref, out_ref):
        gather_blocks(devices, length, columns, corner, flat_ref, rows_ref, t_ref, out_ref)

    return pl.pallas_call(
        kernel,
        out_shape=pltpu.VMEM((devices // 4, columns, per), jnp.float32),
        in_specs=[vmem, smem, vmem],
        compiler_params=pltpu.CompilerParams(vmem_limit_bytes=VMEM_GRANT),
    )(in_space(table, pltpu.VMEM), in_space(flat, pltpu.SMEM), in_space(rows, pltpu.VMEM))


def times(left, right):
    return lax.dot_general(left, right, (((1,), (1,)), ((), ())), precision=lax.Precision.HIGHEST)


def on_chip(kernel, shape, *operands):
    return pl.pallas_call(
        kernel,
        out_shape=pltpu.VMEM(shape, jnp.float32),
        in_specs=[pl.BlockSpec(memory_space=pltpu.VMEM)] * len(operands),
        compiler_params=pltpu.CompilerParams(vmem_limit_bytes=VMEM_GRANT),
    )(*(in_space(a, pltpu.VMEM) for a in operands))


def square(full):
    blocks, columns, _ = full.shape

    def kernel(a_ref, o_ref):
        o_ref[...] = sum(times(a_ref[i], a_ref[i]) for i in range(blocks))

    return on_chip(kernel, (columns, columns), full)


def products(own, full, other, everything):
    blocks, columns, _ = full.shape

    def kernel(own_ref, a_ref, b_ref, o_ref):
        own = own_ref[...]
        cross = sum(times(a_ref[i], b_ref[i]) for i in range(blocks))
        first = lax.axis_index("col") == 0
        both = jnp.concatenate([jnp.where(first, own, cross), jnp.where(first, cross, own)], axis=1)
        o_ref[...] = both * (1.0 / everything)

    return on_chip(kernel, (columns, 2 * columns), own, full, other)


def swap(value, k):
    size = lax.axis_size("row")
    return lax.ppermute(value, "row", [(i, i ^ (step_of(k, i.bit_count() & 1) if k else 1)) for i in range(size)])


def body(matrix_panel, row_signs, sample_rows):
    devices = lax.axis_size("row")
    columns, _ = matrix_panel.shape
    everything = sample_rows.shape[0]
    bits = devices.bit_length() - 1

    def part(table, c0, c1):
        return pick(table, flat, rows, columns, (c0, c1))

    table, far, flat, rows = mix(matrix_panel, row_signs, sample_rows, devices, (1, 1))
    send = part(table, 0, 1) + swap(far, 0)
    table, send = lax.optimization_barrier((table, send))
    half = send.shape[0] // 2
    first = swap(send[half:], 1)
    second = swap(send[:half], 1)
    far = part(table, 1, 0)
    near = swap(far, 0)
    table, far = lax.optimization_barrier((table, far))
    rest = part(table, 0, 0)
    keep = rest + near
    for k in range(2, bits - 1):
        send = keep[half:] + first
        send, low = lax.optimization_barrier((send, keep[:half]))
        half = half // 2
        if k < bits - 2:
            first, later = swap(send[half:], k), swap(send[:half], k)
            keep = low + second
            second = later
        else:
            moved = swap(send, k)
            keep = low + second
    total = keep + moved
    moved = swap(total, bits - 1)
    mine = total[0] + moved[1]
    theirs = total[1] + moved[0]
    full = jnp.concatenate([mine[None], theirs[None]], axis=0)
    size = lax.axis_size("col")
    around = [(r * size + c, r * size + (c ^ 1)) for r in range(devices) for c in range(size)]
    other = lax.ppermute(full, ("row", "col"), around)
    own = square(full)
    gram = products(own, full, other, everything)
    for k in range(bits - 1):
        gram = gram + lax.ppermute(gram, "row", [(i, i ^ step_of(k, 0)) for i in range(devices)])
    sketch = mine
    return (sketch, gram)


def solution(mesh):
    return jax.shard_map(
        body,
        mesh=mesh,
        in_specs=(P("col", "row"), P("row"), P()),
        out_specs=(P("col", "row"), P("col", None)),
        check_vma=False,
    )
```
